32 devices in a mesh: gx: 8 (over y, x, core), gy: 4 (over z).
Axes of the slice: x: 2, y: 2, z: 4, core: 2. Of those that a mesh axis runs over, the one named last changes fastest.
Arguments:
- src_table: bfloat16 [65536, 256], P(('gx', 'gy')), may hold values from -1.5 to 1.5
- src_acc: float32 [65536], P(('gx', 'gy')), may hold values from 0.02 to 0.5
- dst_table: bfloat16 [65536, 256], P(('gx', 'gy')), may hold values from -1.5 to 1.5
- dst_acc: float32 [65536], P(('gx', 'gy')), may hold values from 0.02 to 0.5
- relations: float32 [16, 256], replicated, may hold values from -4 to 4
- rel_acc: float32 [16], replicated, may hold values from 20 to 200
- edge_src: int32 [8, 4, 2, 512], P('gx', 'gy'), may hold values from 0 to 2047
- edge_dst: int32 [8, 4, 2, 512], P('gx', 'gy'), may hold values from 0 to 2047
- edge_rel: int32 [8, 4, 2, 512], P('gx', 'gy'), may hold values from 0 to 15
- negatives: int32 [8, 4, 2, 1, 512], P('gx', 'gy'), may hold values from 0 to 2047
- counts: int32 [8, 4, 2], P('gx', 'gy'), may hold values from 128 to 512
Outputs:
- src_out: bfloat16 [65536, 256], P(('gx', 'gy'))
- src_acc_out: float32 [65536], P(('gx', 'gy'))
- dst_out: bfloat16 [65536, 256], P(('gx', 'gy'))
- dst_acc_out: float32 [65536], P(('gx', 'gy'))
- relations_out: float32 [16, 256], replicated
The draws below stay inside these ranges and needn't reach their ends.
Inputs may be any that keep to these rules, and one draw needn't show every extreme that they name: `edge_src`: row of the source partition of the bucket. `edge_dst`: row of the destination partition of the bucket. `negatives`: row of the destination partition of the bucket. Only the first counts slots of a bucket's edge lists are live.
All inputs are finite; a program needn't handle non-finite values.
Results may differ from the reference program's by a relative error of at most 0.0027.
Values may be sent and summed in bfloat16 or wider, within the bound.
No kernel may reach another device: no remote copies, remote signals or barrier semaphores. Data moves between devices by JAX's collectives and lax.ppermute only.
A program may use at most 64 MiB of HBM per device.

```python
import math
import jax
import jax.numpy as jnp
from jax import lax

D = 256
NREL = 16
NEG = 512
STEPS = 2
ROWS = 2048
EDGES = 512
NBLK = 1
SRC_ROWS = 65536
N_GX = 8
N_GY = 4


def with_ends(entries, key, least, top_value):
    shape = entries.shape
    place = [jax.random.randint(jax.random.fold_in(key, axis), (), 0, shape[axis]) for axis in range(len(shape))]
    entries = entries.at[tuple(place)].set(least)
    longest = shape.index(max(shape))
    place[longest] = (place[longest] + 1) % shape[longest]
    return entries.at[tuple(place)].set(top_value)


def shard_levels(key, extent, split, smallest, top_value):
    def one(dim, blocks):
        steps = jax.random.uniform(jax.random.fold_in(jax.random.fold_in(key, 6), dim), (blocks,), jnp.float32, smallest / len(split), top_value / len(split))
        return jnp.repeat(jnp.exp(steps), extent[dim] // blocks).reshape((-1,) + (1,) * (len(extent) - dim - 1))

    gain = one(*split[0])
    for cut in split[1:]:
        gain = gain * one(*cut)
    return gain


def noise(stream_key, shape, deviation, most, cuts=(), kind=jnp.bfloat16):
    values = deviation * jax.random.normal(stream_key, shape, jnp.float32)
    if cuts:
        values = values * shard_levels(stream_key, shape, cuts, -0.22, 0.18)
    return jnp.clip(values, -most, most).astype(kind)


def setup_inputs(seed: int = 0) -> dict:
    splits = jax.random.split(jax.random.key(seed), 12)
    return {
        "src_table": noise(splits[0], (SRC_ROWS, D), 0.25, 1.5, ((0, 32),)),
        "src_acc": jnp.clip(jnp.exp(math.log(0.5) - 3.218876 * jax.random.uniform(splits[1], (SRC_ROWS,), jnp.float32) ** shard_levels(splits[1], (SRC_ROWS,), ((0, 32),), -0.2, 0.2)), 0.02, 0.5),
        "dst_table": noise(splits[2], (SRC_ROWS, D), 0.25, 1.5, ((0, 32),)),
        "dst_acc": jnp.clip(jnp.exp(math.log(0.5) - 3.218876 * jax.random.uniform(splits[3], (SRC_ROWS,), jnp.float32) ** shard_levels(splits[3], (SRC_ROWS,), ((0, 32),), -0.2, 0.2)), 0.02, 0.5),
        "relations": noise(splits[4], (NREL, D), 1.0, 4.0, (), jnp.float32),
        "rel_acc": jnp.clip(jnp.exp(jax.random.uniform(splits[5], (NREL,), jnp.float32, math.log(20.0), math.log(200.0))), 20.0, 200.0),
        "edge_src": with_ends(jax.random.randint(splits[6], (N_GX, N_GY, STEPS, EDGES), 0, ROWS), jax.random.fold_in(splits[6], 1), 0, ROWS - 1).astype(jnp.int32),
        "edge_dst": with_ends(jax.random.randint(splits[7], (N_GX, N_GY, STEPS, EDGES), 0, ROWS), jax.random.fold_in(splits[7], 1), 0, ROWS - 1).astype(jnp.int32),
        "edge_rel": with_ends(jax.random.randint(splits[8], (N_GX, N_GY, STEPS, EDGES), 0, NREL), jax.random.fold_in(splits[8], 1), 0, NREL - 1).astype(jnp.int32),
        "negatives": with_ends(jax.random.randint(splits[9], (N_GX, N_GY, STEPS, NBLK, NEG), 0, ROWS), jax.random.fold_in(splits[9], 1), 0, ROWS - 1).astype(jnp.int32),
        "counts": with_ends(jax.random.randint(splits[10], (N_GX, N_GY, STEPS), EDGES // 4, EDGES + 1), jax.random.fold_in(splits[10], 1), EDGES // 4, EDGES).astype(jnp.int32),
    }


learn_rate = 0.1
relation_rate = 0.5

def bucket_grads(source_rows, dest_slab, relations, dest_ids, rel_ids, negative_ids, live_count, block_count):
    edge_total, columns = source_rows.shape
    block_size = edge_total // negative_ids.shape[0]
    negative_weight = negative_ids.shape[1] ** (-0.5)
    rel_total = relations.shape[0]

    def block_step(number, totals):
        edge_grads, dest_grads, rel_grads = totals
        offset = (number * block_size).astype(jnp.int32)
        source = lax.dynamic_slice_in_dim(source_rows, offset, block_size, 0).astype(jnp.float32)
        dest_block = lax.dynamic_slice_in_dim(dest_ids, offset, block_size, 0)
        rel_block = lax.dynamic_slice_in_dim(rel_ids, offset, block_size, 0)
        negative_rows = lax.dynamic_index_in_dim(negative_ids, number, 0, keepdims=False)
        target = jnp.take(dest_slab, dest_block, axis=0).astype(jnp.float32)
        samples = jnp.take(dest_slab, negative_rows, axis=0)
        onehot = (rel_block[:, None] == jnp.arange(rel_total, dtype=jnp.int32)[None, :]).astype(jnp.float32)
        diagonal = jnp.dot(onehot, relations, precision=lax.Precision.HIGHEST, preferred_element_type=jnp.float32)
        live_mask = (offset + jnp.arange(block_size, dtype=jnp.int32) < live_count).astype(jnp.float32)
        rotated = source * diagonal
        rotated_half = rotated.astype(jnp.bfloat16)
        positive = lax.optimization_barrier(jnp.sum(rotated * target, axis=1))
        scores = lax.dot_general(rotated_half, samples, (((1,), (1,)), ((), ())), preferred_element_type=jnp.float32)
        slopes = (live_mask[:, None] * negative_weight * jax.nn.sigmoid(scores)).astype(jnp.bfloat16)
        pulls = -live_mask * jax.nn.sigmoid(-positive)
        pushes = jnp.dot(slopes, samples, preferred_element_type=jnp.float32)
        upstream = pulls[:, None] * target + pushes
        edge_grads = lax.dynamic_update_slice_in_dim(edge_grads, upstream * diagonal, offset, 0)
        sample_grads = lax.dot_general(slopes, rotated_half, (((0,), (0,)), ((), ())), preferred_element_type=jnp.float32)
        dest_grads = dest_grads.at[dest_block].add(pulls[:, None] * rotated).at[negative_rows].add(sample_grads)
        rel_grads = rel_grads + lax.dot_general(onehot, upstream * source, (((0,), (0,)), ((), ())), precision=lax.Precision.HIGHEST, preferred_element_type=jnp.float32)
        return (edge_grads, dest_grads, rel_grads)
    start_totals = (jnp.zeros((edge_total, columns), jnp.float32), jnp.zeros(dest_slab.shape, jnp.float32), jnp.zeros(relations.shape, jnp.float32))
    return lax.fori_loop(0, block_count, block_step, start_totals)

def adagrad(embedding, accumulator, gradient):
    accum_new = accumulator + lax.optimization_barrier(jnp.mean(gradient * gradient, axis=-1))
    moved = embedding.astype(jnp.float32) - learn_rate * gradient / jnp.sqrt(accum_new)[..., None]
    return (moved.astype(jnp.bfloat16), accum_new)

def reference(src_table, src_acc, dst_table, dst_acc, relations, rel_acc, edge_src, edge_dst, edge_rel, negatives, counts):
    source = src_table.reshape(N_GX, N_GY, ROWS, D)
    source_state = src_acc.reshape(N_GX, N_GY, ROWS)
    target = dst_table.reshape(N_GX, N_GY, ROWS, D)
    target_state = dst_acc.reshape(N_GX, N_GY, ROWS)
    devices_all = N_GX * N_GY
    relation_grad = jnp.zeros((NREL, D), jnp.float32)

    def flatten(array):
        return array.reshape((devices_all,) + array.shape[2:])

    def unflatten(array):
        return array.reshape((N_GX, N_GY) + array.shape[1:])

    def device_work(pieces):
        src_slab, src_state, dst_slab, dst_state, src_ids, dst_ids, rel_ids, neg_ids, live_count = pieces
        picked = jnp.take(src_slab, src_ids, axis=0)
        edge_grads, dest_grads, rel_grads = bucket_grads(picked, dst_slab, relations, dst_ids, rel_ids, neg_ids, live_count, NBLK)
        source_grads = jnp.zeros((ROWS, D), jnp.float32).at[src_ids].add(edge_grads)
        new_src, new_src_state = adagrad(src_slab, src_state, source_grads)
        new_dst, new_dst_state = adagrad(dst_slab, dst_state, dest_grads)
        return (new_src, new_src_state, new_dst, new_dst_state, rel_grads)
    for bucket_step in range(STEPS):
        pieces = (flatten(jnp.roll(source, bucket_step, axis=0)), flatten(jnp.roll(source_state, bucket_step, axis=0)), flatten(jnp.roll(target, bucket_step, axis=1)), flatten(jnp.roll(target_state, bucket_step, axis=1)), flatten(edge_src[:, :, bucket_step]), flatten(edge_dst[:, :, bucket_step]), flatten(edge_rel[:, :, bucket_step]), flatten(negatives[:, :, bucket_step]), flatten(counts[:, :, bucket_step]))
        new_src, new_src_state, new_dst, new_dst_state, rel_grads = lax.map(device_work, pieces)
        source = jnp.roll(unflatten(new_src), -bucket_step, axis=0)
        source_state = jnp.roll(unflatten(new_src_state), -bucket_step, axis=0)
        target = jnp.roll(unflatten(new_dst), -bucket_step, axis=1)
        target_state = jnp.roll(unflatten(new_dst_state), -bucket_step, axis=1)
        relation_grad = relation_grad + lax.optimization_barrier(jnp.sum(rel_grads, axis=0))
    relation_state = rel_acc + lax.optimization_barrier(jnp.mean(relation_grad * relation_grad, axis=1))
    relations_out = relations - relation_rate * relation_grad / jnp.sqrt(relation_state)[:, None]
    return (source.reshape(SRC_ROWS, D), source_state.reshape(SRC_ROWS), target.reshape(SRC_ROWS, D), target_state.reshape(SRC_ROWS), relations_out)
```

```python
import functools

import jax
import jax.numpy as jnp
from jax import lax
from jax.experimental import pallas as pl
from jax.experimental.pallas import tpu as pltpu
from jax.sharding import PartitionSpec as P

learn_rate = 0.1
relation_rate = 0.5
LANES = 128
CHUNK = 512
f32 = jnp.float32
bf16 = jnp.bfloat16
i32 = jnp.int32
AXES = ("gx", "gy")


def dot(a, b, ca=1, cb=0):
    return lax.dot_general(a, b, (((ca,), (cb,)), ((), ())), preferred_element_type=f32)


def hot_lanes(column, total):
    n = column.shape[0]
    return (column == lax.broadcasted_iota(i32, (n, total), 1)).astype(f32).astype(bf16)


def hot_sublanes(row, start, total):
    n = row.shape[1]
    return (row == lax.broadcasted_iota(i32, (total, n), 0) + start).astype(f32).astype(bf16)


def eye():
    shape = (LANES, LANES)
    return lax.broadcasted_iota(i32, shape, 0) == lax.broadcasted_iota(i32, shape, 1)


def to_column(row):
    diagonal = eye()
    zero = jnp.zeros((), row.dtype)
    parts = [
        jnp.sum(jnp.where(diagonal, row[:, k : k + LANES], zero), axis=1, keepdims=True)
        for k in range(0, row.shape[1], LANES)
    ]
    return parts[0] if len(parts) == 1 else jnp.concatenate(parts, axis=0)


def id_column(row):
    return to_column(row.astype(f32)).astype(i32)


def split_relations(relations):
    high = relations.astype(bf16)
    rest = relations - high.astype(f32)
    middle = rest.astype(bf16)
    low = (rest - middle.astype(f32)).astype(bf16)
    return jnp.concatenate([high, middle, low], axis=0)


def bucket_math(source, target, samples, relations, rel_row, live_count, blocks):
    edges, columns = source.shape
    kinds = relations.shape[0]
    size = edges // blocks
    shared = samples.shape[0] // blocks
    weight = shared**-0.5
    rel_col = id_column(rel_row)
    lanes = lax.broadcasted_iota(i32, (edges, 3 * kinds), 1)
    third = jnp.where(lanes < kinds, lanes, jnp.where(lanes < 2 * kinds, lanes - kinds, lanes - 2 * kinds))
    pick = (rel_col == third).astype(f32).astype(bf16)
    diagonal = dot(pick, split_relations(relations))
    live = (lax.broadcasted_iota(i32, (edges, 1), 0) < live_count).astype(f32)
    rotated = source * diagonal
    rotated_half = rotated.astype(bf16)
    positive = jnp.sum(rotated * target, axis=1, keepdims=True)
    pulls = -live * jax.nn.sigmoid(-positive)
    slopes, pushes = [], []
    for b in range(blocks):
        rows = slice(b * size, (b + 1) * size)
        negatives = samples[b * shared : (b + 1) * shared]
        scores = dot(rotated_half[rows], negatives, 1, 1)
        slope = (live[rows] * weight * jax.nn.sigmoid(scores)).astype(bf16)
        slopes.append(slope)
        pushes.append(dot(slope, negatives))
    slope = slopes[0] if blocks == 1 else jnp.concatenate(slopes, axis=0)
    push = pushes[0] if blocks == 1 else jnp.concatenate(pushes, axis=0)
    upstream = pulls * target + push
    edge_grads = (upstream * diagonal).astype(bf16)
    pulled = (pulls * rotated).astype(bf16)
    product = upstream * source
    high = product.astype(bf16)
    low = (product - high.astype(f32)).astype(bf16)
    sort = hot_sublanes(rel_row, 0, kinds)
    rel_grads = dot(sort, high) + dot(sort, low)
    return edge_grads, slope, rotated_half, pulled, rel_grads


def row_update(table_ref, acc_ref, out_ref, acc_out_ref, ids_row, values):
    total, columns = table_ref.shape
    diagonal = eye()
    for start in range(0, total, CHUNK):
        size = min(CHUNK, total - start)
        grads = dot(hot_sublanes(ids_row, start, size), values)
        mean = jnp.sum(grads * grads, axis=1, keepdims=True) * (1.0 / columns)
        scales = []
        for k in range(0, size, LANES):
            at = (start + k) // LANES
            before = to_column(acc_ref[at : at + 1, :])
            after = before + mean[k : k + LANES]
            acc_out_ref[at : at + 1, :] = jnp.sum(jnp.where(diagonal, after, 0.0), axis=0, keepdims=True)
            scales.append(learn_rate / jnp.sqrt(after))
        scale = jnp.concatenate(scales, axis=0)
        moved = table_ref[start : start + size, :].astype(f32) - grads * scale
        out_ref[start : start + size, :] = moved.astype(bf16)


def dest_values(slope, rotated_half, pulled, blocks):
    size = slope.shape[0] // blocks
    parts = [pulled]
    for b in range(blocks):
        rows = slice(b * size, (b + 1) * size)
        parts.append(dot(slope[rows], rotated_half[rows], 0, 0).astype(bf16))
    return jnp.concatenate(parts, axis=0)


def first_kernel(
    blocks,
    src_ref, src_acc_ref, dst_ref, rel_ref, es_ref, ed_ref, er_ref, ng_ref, cnt_ref, next_ref,
    src_out, acc_out, rows_out, slope_out, rot_out, pull_out, relg_out,
):
    total = src_ref.shape[0]
    src_row, dst_row, rel_row = es_ref[0, 0, 0:1, :], ed_ref[0, 0, 0:1, :], er_ref[0, 0, 0:1, :]
    source = dot(hot_lanes(id_column(src_row), total), src_ref[...])
    target = dot(hot_lanes(id_column(dst_row), total), dst_ref[...])
    samples = jnp.concatenate(
        [dot(hot_lanes(id_column(ng_ref[0, 0, 0, b : b + 1, :]), total), dst_ref[...]).astype(bf16) for b in range(blocks)],
        axis=0,
    )
    edge_grads, slope, rotated_half, pulled, rel_grads = bucket_math(
        source, target, samples, rel_ref[...], rel_row, cnt_ref[0, 0, 0], blocks
    )
    slope_out[...] = slope
    rot_out[...] = rotated_half
    pull_out[...] = pulled
    relg_out[...] = rel_grads
    row_update(src_ref, src_acc_ref, src_out, acc_out, src_row, edge_grads)
    next_row = next_ref[0, 0, 1:2, :]
    rows_out[...] = dot(hot_lanes(id_column(next_row), total), src_out[...]).astype(bf16)


def dest_kernel(
    blocks,
    dst_ref, acc_ref, ed_ref, ng_ref, slope_ref, rot_ref, pull_ref, ids_ref,
    dst_out, acc_out, target_out, sample_out,
):
    total = dst_ref.shape[0]
    values = dest_values(slope_ref[...], rot_ref[...], pull_ref[...], blocks)
    ids = jnp.concatenate(
        [ed_ref[0, 0, 0:1, :]] + [ng_ref[0, 0, 0, b : b + 1, :] for b in range(blocks)], axis=1
    )
    row_update(dst_ref, acc_ref, dst_out, acc_out, ids, values)
    edges = ed_ref.shape[3]
    table = dst_out[...]
    target_out[...] = dot(hot_lanes(id_column(ids_ref[0:1, :edges]), total), table).astype(bf16)
    count = sample_out.shape[0]
    sample_out[...] = dot(hot_lanes(id_column(ids_ref[2:3, :count]), total), table).astype(bf16)


def second_kernel(
    blocks,
    rows_ref, target_ref, sample_ref, rel_ref, ids_ref, early_ref,
    edge_out, slope_out, rot_out, pull_out, relg_out,
):
    edges = rows_ref.shape[0]
    edge_grads, slope, rotated_half, pulled, rel_grads = bucket_math(
        rows_ref[...].astype(f32),
        target_ref[...].astype(f32),
        sample_ref[...],
        rel_ref[...],
        ids_ref[1:2, :edges],
        ids_ref[3:4, 0:1],
        blocks,
    )
    edge_out[...] = edge_grads
    slope_out[...] = slope
    rot_out[...] = rotated_half
    pull_out[...] = pulled
    relg_out[...] = rel_grads + early_ref[...]


def dest_last_kernel(blocks, dst_ref, acc_ref, slope_ref, rot_ref, pull_ref, ids_ref, dst_out, acc_out):
    values = dest_values(slope_ref[...], rot_ref[...], pull_ref[...], blocks)
    edges = pull_ref.shape[0]
    count = values.shape[0] - edges
    ids = jnp.concatenate([ids_ref[0:1, :edges], ids_ref[2:3, :count]], axis=1)
    row_update(dst_ref, acc_ref, dst_out, acc_out, ids, values)


def source_last_kernel(src_ref, acc_ref, edge_ref, next_ref, src_out, acc_out):
    row_update(src_ref, acc_ref, src_out, acc_out, next_ref[0, 0, 1:2, :], edge_ref[...])


def call(body, outs, smem=(), count=0):
    def spec(i):
        return pl.BlockSpec(memory_space=pltpu.SMEM if i in smem else pltpu.VMEM)

    return pl.pallas_call(
        body,
        out_shape=[jax.ShapeDtypeStruct(s, d) for s, d in outs],
        in_specs=[spec(i) for i in range(count)],
        out_specs=[pl.BlockSpec(memory_space=pltpu.VMEM) for _ in outs],
    )


def shifted(x, gx_by, gy_by):
    nx, ny = lax.axis_size("gx"), lax.axis_size("gy")
    pairs = [
        (i * ny + j, ((i + gx_by) % nx) * ny + (j + gy_by) % ny) for i in range(nx) for j in range(ny)
    ]
    return lax.ppermute(x, AXES, pairs)


def sum_everywhere(x):
    for axis in AXES:
        peers = lax.axis_size(axis)
        if peers & (peers - 1):
            x = lax.psum(x, axis)
            continue
        step = 1
        while step < peers:
            x = x + lax.ppermute(x, axis, [(i, i ^ step) for i in range(peers)])
            step *= 2
    return x


def local(
    src_table, src_acc, dst_table, dst_acc, relations, rel_acc,
    edge_src, edge_dst, edge_rel, negatives, counts,
):
    total, columns = src_table.shape
    edges = edge_src.shape[3]
    blocks, shared = negatives.shape[3:]
    kinds = relations.shape[0]
    width = max(edges, blocks * shared)
    src_acc = src_acc.reshape(-1, LANES)
    dst_acc = dst_acc.reshape(-1, LANES)
    next_src = shifted(edge_src, -1, 0)

    def wide(x):
        return jnp.pad(x, (0, width - x.shape[0]))

    packed = jnp.stack(
        [
            wide(edge_dst[0, 0, 1]),
            wide(edge_rel[0, 0, 1]),
            wide(negatives[0, 0, 1].reshape(-1)),
            jnp.broadcast_to(counts[0, 0, 1], (width,)),
        ]
    )
    next_ids = shifted(packed, 0, -1)
    slab = ((total, columns), bf16)
    state = (src_acc.shape, f32)
    sums = [((edges, shared), bf16), ((edges, columns), bf16), ((edges, columns), bf16), ((kinds, columns), f32)]
    rows_shape = ((edges, columns), bf16)
    src_mid, src_state, rows, slope, rot, pull, early = call(
        functools.partial(first_kernel, blocks), [slab, state, rows_shape] + sums, smem=(8,), count=10
    )(src_table, src_acc, dst_table, relations, edge_src, edge_dst, edge_rel, negatives, counts, next_src)
    there = shifted(rows, 1, -1)
    dst_mid, dst_state, target, samples = call(
        functools.partial(dest_kernel, blocks),
        [slab, state, rows_shape, ((blocks * shared, columns), bf16)],
        count=8,
    )(dst_table, dst_acc, edge_dst, negatives, slope, rot, pull, next_ids)
    edge_grads, slope, rot, pull, both = call(
        functools.partial(second_kernel, blocks), [rows_shape] + sums, count=6
    )(there, target, samples, relations, next_ids, early)
    home = shifted(edge_grads, -1, 1)
    relation_grad = sum_everywhere(both)
    dst_out, dst_acc_out = call(
        functools.partial(dest_last_kernel, blocks), [slab, state], count=6
    )(dst_mid, dst_state, slope, rot, pull, next_ids)
    src_out, src_acc_out = call(source_last_kernel, [slab, state], count=4)(src_mid, src_state, home, next_src)
    relation_state = rel_acc + jnp.mean(relation_grad * relation_grad, axis=1)
    relations_out = relations - relation_rate * relation_grad / jnp.sqrt(relation_state)[:, None]
    return (src_out, src_acc_out.reshape(-1), dst_out, dst_acc_out.reshape(-1), relations_out)


def solution(mesh):
    placed = (
        P(AXES, None), P(AXES), P(AXES, None), P(AXES), P(), P(),
        P("gx", "gy", None, None), P("gx", "gy", None, None), P("gx", "gy", None, None),
        P("gx", "gy", None, None, None), P("gx", "gy", None),
    )
    return jax.shard_map(
        local,
        mesh=mesh,
        in_specs=placed,
        out_specs=(P(AXES, None), P(AXES), P(AXES, None), P(AXES), P()),
        check_vma=False,
    )
```
